32 devices in a mesh: groups: 2 (over x), view: 16 (over z, y, core).
Axes of the slice: x: 2, y: 2, z: 4, core: 2. Of those that a mesh axis runs over, the one named last changes fastest.
Arguments:
- query: bfloat16 [4096, 1024], P(('groups', 'view')), parts along dimension 0, may hold values from -28 to 28
- keys: bfloat16 [4096, 1024], P(('groups', 'view')), parts along dimension 0, may hold values from -6 to 6
- values: bfloat16 [4096, 1024], P(('groups', 'view')), parts along dimension 0, may hold values from -6 to 6
- grad_out: bfloat16 [4096, 1024], P(('groups', 'view')), parts along dimension 0, may hold values from -6 to 6
- margin: int32 [32, 4, 1, 1], P('groups'), parts along dimension 0, may hold values 0 or 1
Outputs:
- attended: bfloat16 [4096, 1024], P(('groups', 'view')), parts along dimension 0
- grad_query: bfloat16 [4096, 1024], P(('groups', 'view')), parts along dimension 0
- grad_key: bfloat16 [4096, 1024], P(('groups', 'view')), parts along dimension 0
- grad_value: bfloat16 [4096, 1024], P(('groups', 'view')), parts along dimension 0
The draws below stay inside these ranges and needn't reach their ends.
There are 2 independent parts, one for each index of `groups`. The reference program is written for one: setup_inputs(seed, part) draws one part's arguments, and reference() takes and returns one part's arrays. A program takes and returns all parts, laid end to end along the dimension named above; each array names one. Nothing has to cross between parts.
All inputs are finite; a program needn't handle non-finite values.
Results may differ from the reference program's by a relative error of at most 0.033.
Values may be sent and summed in bfloat16 or wider, within the bound.
No kernel may reach another device: no remote copies, remote signals or barrier semaphores. Data moves between devices by JAX's collectives and lax.ppermute only.
A program may use at most 64 MiB of HBM per device.

```python
import math
import jax
import jax.numpy as jnp
from jax import lax

H = 8
DH = 128
HW = 1024
IMG_TOK = 128
BLK = 128
NB = 1
SPAN = 2
IMAGES = 16
ROWS = 2048


def drawn_pair(key):
    base = jax.random.fold_in(key, 7)
    first, second = jax.random.split(base, 2)
    shape = (IMAGES, IMG_TOK, HW)
    query_draw = jax.random.truncated_normal(first, -6.0, 6.0, shape, jnp.float32)
    key_draw = jax.random.truncated_normal(second, -6.0, 6.0, shape, jnp.float32)
    return (query_draw.reshape(ROWS, HW), key_draw.reshape(ROWS, HW))


def draw_query(key, part):
    return drawn_pair(key)[0].astype(jnp.bfloat16)


def draw_keys(key, part):
    return drawn_pair(key)[1].astype(jnp.bfloat16)


def plant(drawn, key, least, high):
    dims = drawn.shape
    place = [jax.random.randint(jax.random.fold_in(key, axis), (), 0, dims[axis]) for axis in range(len(dims))]
    drawn = drawn.at[tuple(place)].set(least)
    longest = dims.index(max(dims))
    place[longest] = (place[longest] + 1) % dims[longest]
    return drawn.at[tuple(place)].set(high)


def block_scale(key, shape, shards, least, top_value):
    loudness, own = 1.0, jax.random.fold_in(key, 6)
    for position, blocks in shards:
        heights = jnp.exp(jax.random.uniform(jax.random.fold_in(own, position), (blocks,), jnp.float32, least / len(shards), top_value / len(shards)))
        loudness = loudness * jnp.repeat(heights, shape[position] // blocks).reshape([-1 if axis == position else 1 for axis in range(len(shape))])
    return loudness


def bell_draw(key, shape, width, limit, shards=(), held_as=jnp.bfloat16):
    entries = width * jax.random.normal(key, shape, jnp.float32)
    if shards:
        entries = entries * block_scale(key, shape, shards, -0.22, 0.18)
    return jnp.clip(entries, -limit, limit).astype(held_as)


def setup_inputs(seed: int = 0, part: int = 0) -> dict:
    key_of = jax.random.split(jax.random.key(seed), 6)
    part_keys = jax.random.split(jax.random.fold_in(key_of[5], part), 6)
    query = draw_query(jax.random.fold_in(jax.random.fold_in(key_of[5], part), 71), part)
    keys = draw_keys(jax.random.fold_in(jax.random.fold_in(key_of[5], part), 71), part)
    values = bell_draw(part_keys[2], (ROWS, HW), 1.0, 6.0, ((0, 16),))
    grad_out = bell_draw(part_keys[3], (ROWS, HW), 1.0, 6.0, ((0, 16),))
    margin = plant((jax.random.randint(part_keys[4], (IMAGES, 2 * SPAN, NB, NB), 0, 3) < 1).astype(jnp.int32), jax.random.fold_in(part_keys[4], 1), 0, 1)
    return {"query": query, "keys": keys, "values": values, "grad_out": grad_out, "margin": margin}


NEG_FILL = -1e+30

def allowed_grid(margin, image_index):
    mask_row = lax.dynamic_index_in_dim(margin, image_index, 0, keepdims=False)
    filled = jnp.ones((1, NB, NB), mask_row.dtype)
    mask_spans = jnp.concatenate([mask_row[:SPAN], filled, mask_row[SPAN:]], axis=0)
    block_grid = jnp.transpose(mask_spans, (1, 0, 2)).reshape(NB, (2 * SPAN + 1) * NB)
    return jnp.repeat(jnp.repeat(block_grid, BLK, axis=0), BLK, axis=1) > 0

def reference(query, keys, values, grad_out, margin):
    query_images = query.reshape(IMAGES, IMG_TOK, H, DH)
    key_images = keys.reshape(IMAGES, IMG_TOK, H, DH)
    value_images = values.reshape(IMAGES, IMG_TOK, H, DH)
    grad_images = grad_out.reshape(IMAGES, IMG_TOK, H, DH)
    score_scale = 1.0 / math.sqrt(DH)
    shifts = jnp.arange(-SPAN, SPAN + 1, dtype=jnp.int32)

    def visit(running, image_index):
        key_acc, value_acc = running
        neighbours = ((image_index + shifts) % IMAGES).astype(jnp.int32)
        key_all = jnp.take(key_images, neighbours, axis=0).reshape(-1, H, DH).astype(jnp.float32)
        value_all = jnp.take(value_images, neighbours, axis=0).reshape(-1, H, DH).astype(jnp.float32)
        query_here = lax.dynamic_index_in_dim(query_images, image_index, 0, keepdims=False).astype(jnp.float32)
        grad_here = lax.dynamic_index_in_dim(grad_images, image_index, 0, keepdims=False).astype(jnp.float32)
        allowed = allowed_grid(margin, image_index)
        scores = jnp.einsum('qhd,khd->hqk', query_here, key_all) * score_scale
        scores = jnp.where(allowed[None], scores, NEG_FILL)
        row_max = lax.optimization_barrier(jnp.max(scores, axis=-1, keepdims=True))
        log_total = row_max + jnp.log(lax.optimization_barrier(jnp.sum(jnp.exp(scores - row_max), axis=-1, keepdims=True)))
        prob_full = jnp.exp(scores - log_total)
        prob_half = lax.optimization_barrier(prob_full.astype(jnp.bfloat16)).astype(jnp.float32)
        attended = jnp.einsum('hqk,khd->qhd', prob_half, value_all).astype(jnp.bfloat16)
        row_dot = lax.optimization_barrier(jnp.sum(grad_here * attended.astype(jnp.float32), axis=-1))
        row_dot = jnp.transpose(row_dot)[..., None]
        prob_grad = jnp.einsum('qhd,khd->hqk', grad_here, value_all)
        grad_half = lax.optimization_barrier((prob_full * (prob_grad - row_dot)).astype(jnp.bfloat16)).astype(jnp.float32)
        grad_query = (jnp.einsum('hqk,khd->qhd', grad_half, key_all) * score_scale).astype(jnp.bfloat16)
        key_terms = jnp.einsum('hqk,qhd->khd', grad_half, query_here).reshape(2 * SPAN + 1, IMG_TOK, H, DH)
        value_terms = jnp.einsum('hqk,qhd->khd', prob_half, grad_here).reshape(2 * SPAN + 1, IMG_TOK, H, DH)
        for pair_index in range(2 * SPAN + 1):
            target = neighbours[pair_index]
            key_acc = key_acc.at[target].add(key_terms[pair_index])
            value_acc = value_acc.at[target].add(value_terms[pair_index])
        return ((key_acc, value_acc), (attended, grad_query))
    empty = jnp.zeros((IMAGES, IMG_TOK, H, DH), jnp.float32)
    (key_acc, value_acc), (attended, grad_query) = lax.scan(visit, (empty, empty), jnp.arange(IMAGES, dtype=jnp.int32))
    grad_key = (key_acc * score_scale).astype(jnp.bfloat16).reshape(ROWS, HW)
    grad_value = value_acc.astype(jnp.bfloat16).reshape(ROWS, HW)
    return (attended.reshape(ROWS, HW), grad_query.reshape(ROWS, HW), grad_key, grad_value)
```

```python
import functools
import math

import jax
import jax.numpy as jnp
from jax import lax
from jax.experimental import pallas as pl
from jax.experimental.pallas import tpu as pltpu
from jax.sharding import PartitionSpec as P

H = 8
NEG = -1e30

NT = (((1,), (1,)), ((), ()))
NN = (((1,), (0,)), ((), ()))


def dot(a, b, dims):
    return lax.dot_general(a, b, dims, preferred_element_type=jnp.float32)


def roles(i):
    core, pair = i % 2, (i // 2) % 2
    d_core = 1 - 2 * core
    d_pair = 2 - 4 * pair
    return d_core, d_pair, -d_pair, -d_core


def move(x, source_of):
    n = lax.axis_size("view")
    return lax.ppermute(x, "view", [(source_of(i) % n, i) for i in range(n)])


def from_core(x):
    return move(x, lambda i: i ^ 1)


def from_pair(x):
    return move(x, lambda i: i ^ 2)


def from_far(x):
    return move(x, lambda i: i + (4 if (i // 2) % 2 else -4))


def flag(margin_ref, place, d):
    reach = margin_ref.shape[0] // 2
    o = jnp.where(d < 0, d + reach, d + reach - 1)
    return jnp.where(margin_ref[o, place] > 0, 0.0, NEG)


def row_kernel(scale, images, pos_ref, margin_ref, q_ref, k_ref, v_ref, g_ref, kc_ref, vc_ref, p_ref, z_ref, n_ref, *rest):
    att_ref, gq_ref, st_ref = rest[-3:]
    i = pos_ref[0]
    bias = [0.0] + [flag(margin_ref, i, d) for d in roles(i)]
    q, g = q_ref[...], g_ref[...]
    t = q.shape[0]
    k = jnp.concatenate([k_ref[...], kc_ref[...], p_ref[0], z_ref[0], n_ref[0]], axis=0)
    v = jnp.concatenate([v_ref[...], vc_ref[...], p_ref[1], z_ref[1], n_ref[1]], axis=0)
    s = dot(q, k, NT)
    s = jnp.concatenate([s[:, j * t : (j + 1) * t] * scale + bias[j] for j in range(5)], axis=1)
    m = jnp.max(s, axis=1, keepdims=True)
    e = jnp.exp(s - m)
    total = jnp.sum(e, axis=1, keepdims=True)
    prob = e * (1.0 / total)
    att = dot(prob.astype(jnp.bfloat16), v, NN).astype(jnp.bfloat16)
    att_ref[...] = att
    row = jnp.sum(g.astype(jnp.float32) * att.astype(jnp.float32), axis=1, keepdims=True)
    pg = dot(g, v, NT)
    gh = (prob * (pg - row)).astype(jnp.bfloat16)
    gq_ref[...] = (dot(gh, k, NN) * scale).astype(jnp.bfloat16)
    log_total = m + jnp.log(total)
    lane = lax.broadcasted_iota(jnp.int32, (t, 128), 1)
    both = jnp.where(lane == 0, log_total, row)
    st_ref[0] = jnp.transpose(both)[:8]


def col_kernel(scale, images, pos_ref, margin_ref, k_ref, v_ref, q_ref, g_ref, qc_ref, gc_ref, p_ref, z_ref, n_ref,
               so_ref, sc_ref, sp_ref, sz_ref, sn_ref, *rest):
    gk_ref, gv_ref = rest[-2:]
    i = pos_ref[0]
    bias = [0.0]
    for d in roles(i):
        place = i + d
        place = jnp.where(place < 0, place + images, jnp.where(place >= images, place - images, place))
        bias.append(flag(margin_ref, place, -d))
    k, v = k_ref[...], v_ref[...]
    q = jnp.concatenate([q_ref[...], qc_ref[...], p_ref[0], z_ref[0], n_ref[0]], axis=0)
    g = jnp.concatenate([g_ref[...], gc_ref[...], p_ref[1], z_ref[1], n_ref[1]], axis=0)
    stats = [r[0] for r in (so_ref, sc_ref, sp_ref, sz_ref, sn_ref)]
    log_total = jnp.concatenate([st[0:1] - b for st, b in zip(stats, bias)], axis=1)
    row = jnp.concatenate([st[1:2] for st in stats], axis=1)
    s = dot(k, q, NT) * scale
    prob = jnp.exp(s - log_total)
    gv_ref[...] = dot(prob.astype(jnp.bfloat16), g, NN).astype(jnp.bfloat16)
    pg = dot(v, g, NT)
    gh = (prob * (pg - row)).astype(jnp.bfloat16)
    gk_ref[...] = (dot(gh, q, NN) * scale).astype(jnp.bfloat16)


SMEM = pl.BlockSpec(memory_space=pltpu.SMEM)
ANY = pl.BlockSpec(memory_space=pl.ANY)


def call(kernel, name, first, heads, tokens, head_dim, whole, pairs, stats, outs, carried, stat_out, pos, margin):
    own = pl.BlockSpec((tokens, head_dim), lambda h: (0, h + first))
    two = pl.BlockSpec((2, tokens, head_dim), lambda h: (0, 0, h))
    stat = pl.BlockSpec((1, 8, tokens), lambda h: (h, 0, 0))
    args = [pos, margin, *whole, *pairs, *stats]
    specs = [SMEM, SMEM] + [own] * len(whole) + [two] * len(pairs) + [stat] * len(stats)
    aliases = {}
    if carried:
        for n, c in enumerate(carried):
            aliases[len(args)] = n
            args.append(c)
            specs.append(ANY)
    shapes = [jax.ShapeDtypeStruct(whole[0].shape, jnp.bfloat16)] * outs
    out_specs = [own] * outs
    if stat_out:
        shapes.append(jax.ShapeDtypeStruct((heads, 8, tokens), jnp.float32))
        out_specs.append(stat)
    cols = 5 * tokens
    return pl.pallas_call(
        kernel,
        name=name,
        grid=(heads,),
        in_specs=specs,
        out_specs=out_specs,
        out_shape=shapes,
        input_output_aliases=aliases,
        compiler_params=pltpu.CompilerParams(vmem_limit_bytes=16 << 20),
        cost_estimate=pl.CostEstimate(
            flops=heads * 8 * tokens * cols * head_dim,
            transcendentals=heads * tokens * cols,
            bytes_accessed=heads * tokens * head_dim * 2 * 14,
        ),
    )(*args)


def body(query, keys, values, grad_out, margin):
    tokens, width = query.shape
    head_dim = width // H
    scale = 1.0 / math.sqrt(head_dim)
    images = margin.shape[0]
    position = lax.axis_index("view")
    pos = position.reshape(1).astype(jnp.int32)
    margin_t = jnp.transpose(margin, (1, 2, 3, 0)).reshape(margin.shape[1], images)
    hand_pair = (position % 2) == ((position // 2) % 2)

    def cut(x, y, first, heads):
        c = slice(first * head_dim, (first + heads) * head_dim)
        return jnp.stack((x[:, c], y[:, c]))

    def spread(piece):
        pair = from_pair(piece)
        far = from_far(pair)
        near = from_core(jnp.where(hand_pair, pair, far))
        return pair, far, near

    def spread_stats(st):
        return (
            from_core(st),
            from_pair(st),
            move(st, lambda i: i + (2 if (i // 2) % 2 else -2)),
            move(st, lambda i: i + (1 if i % 2 else -1)),
        )

    row_groups = ((0, 4), (4, 4))
    col_groups = ((0, 4), (4, 2), (6, 2))
    kv = [spread(cut(keys, values, f, n)) for f, n in row_groups]
    kc, vc = from_core(keys), from_core(values)
    qg = [spread(cut(query, grad_out, f, n)) for f, n in col_groups]
    qc, gc = from_core(query), from_core(grad_out)

    carried = None
    stats = {}
    for (f, n), pieces in zip(row_groups, kv):
        att, gq, st = call(
            functools.partial(row_kernel, scale, images), "rows%d" % f, f, n, tokens, head_dim,
            (query, keys, values, grad_out, kc, vc), pieces, (), 2, carried, True, pos, margin_t,
        )
        carried = (att, gq)
        stats[(f, n)] = (st, *spread_stats(st))

    carried_kv = None
    for (f, n), pieces in zip(col_groups, qg):
        for (rf, rn), st in stats.items():
            if rf <= f < rf + rn:
                mine = tuple(x[f - rf : f - rf + n] for x in st)
        gk, gv = call(
            functools.partial(col_kernel, scale, images), "cols%d" % f, f, n, tokens, head_dim,
            (keys, values, query, grad_out, qc, gc), pieces, mine, 2, carried_kv, False, pos, margin_t,
        )
        carried_kv = (gk, gv)
    return (*carried, *carried_kv)


def solution(mesh):
    rows = P(("groups", "view"), None)
    return jax.shard_map(
        body,
        mesh=mesh,
        in_specs=(rows, rows, rows, rows, P("groups", None, None, None)),
        out_specs=(rows, rows, rows, rows),
        check_vma=False,
    )
```
